32 devices in a mesh: fsdp: 8 (over z, y), tp: 4 (over x, core).
Axes of the slice: x: 2, y: 2, z: 4, core: 2. Of those that a mesh axis runs over, the one named last changes fastest.
Arguments:
- tokens: bfloat16 [12544, 768], P(('fsdp', 'tp')), may hold values from -24 to 24
- cotangent: bfloat16 [12544, 768], P(('fsdp', 'tp')), may hold values from -6 to 6
- ln_gain: float32 [3, 768], P(None, ('fsdp', 'tp')), may hold values from 0.1 to 1.9
- ln_bias: float32 [3, 768], P(None, ('fsdp', 'tp')), may hold values from -3 to 3
- out_bias: float32 [3, 768], P(None, ('fsdp', 'tp')), may hold values from -3 to 3
- qv_bias: float32 [4, 768], P(None, ('fsdp', 'tp')), may hold values from -3 to 3
- up_bias: float32 [3072], P(('fsdp', 'tp')), may hold values from -3 to 3
- qkv_spatial: bfloat16 [3, 768, 768], P(None, 'fsdp', 'tp'), may hold values from -0.21875 to 0.21875
- out_spatial: bfloat16 [768, 768], P('tp', 'fsdp'), may hold values from -0.625 to 0.625
- qkv_temporal: bfloat16 [3, 768, 768], P(None, 'fsdp', 'tp'), may hold values from -0.21875 to 0.21875
- out_temporal: bfloat16 [768, 768], P('tp', 'fsdp'), may hold values from -0.3125 to 0.3125
- up_weight: bfloat16 [768, 3072], P('fsdp', 'tp'), may hold values from -0.21875 to 0.21875
- down_weight: bfloat16 [3072, 768], P('tp', 'fsdp'), may hold values from -0.109375 to 0.109375
Outputs:
- output: bfloat16 [12544, 768], P(('fsdp', 'tp'))
- input_grad: float32 [12544, 768], P(('fsdp', 'tp'))
- ln_gain_grad: float32 [3, 768], P(None, ('fsdp', 'tp'))
- ln_bias_grad: float32 [3, 768], P(None, ('fsdp', 'tp'))
- out_bias_grad: float32 [3, 768], P(None, ('fsdp', 'tp'))
- qv_bias_grad: float32 [4, 768], P(None, ('fsdp', 'tp'))
- up_bias_grad: float32 [3072], P(('fsdp', 'tp'))
- qkv_spatial_grad: float32 [3, 768, 768], P(None, 'fsdp', 'tp')
- out_spatial_grad: float32 [768, 768], P('tp', 'fsdp')
- qkv_temporal_grad: float32 [3, 768, 768], P(None, 'fsdp', 'tp')
- out_temporal_grad: float32 [768, 768], P('tp', 'fsdp')
- up_weight_grad: float32 [768, 3072], P('fsdp', 'tp')
- down_weight_grad: float32 [3072, 768], P('tp', 'fsdp')
- root_means: float32 [4], replicated
The draws below stay inside these ranges and needn't reach their ends.
All inputs are finite; a program needn't handle non-finite values.
Results may differ from the reference program's by a relative error of at most 0.018.
Values may be sent and summed in bfloat16 or wider, within the bound.
No kernel may reach another device: no remote copies, remote signals or barrier semaphores. Data moves between devices by JAX's collectives and lax.ppermute only.
A program may use at most 192 MiB of HBM per device.

```python
import jax
import jax.numpy as jnp
from jax import lax

D = 768
HEADS = 12
HD = 64
FF = 3072
FRAMES = 8
PLACES = 196
CLIPS = 2
TOKENS = 12544
N_FSDP = 8


def draw_tokens(key, part):
    row_count = CLIPS * FRAMES * PLACES * N_FSDP // 2
    clip_count = CLIPS * N_FSDP // 2
    noise_key, common_key = jax.random.split(key)
    row_index = jnp.arange(row_count, dtype=jnp.int32)
    position = row_index.astype(jnp.float32) / max(row_count - 1, 1)
    clip_id = row_index // (CLIPS * FRAMES * PLACES) * CLIPS + row_index // (FRAMES // 2 * PLACES) % CLIPS
    noise_part = jax.random.truncated_normal(noise_key, -4.0, 4.0, (row_count, D), jnp.float32)
    common = jax.random.truncated_normal(common_key, -4.0, 4.0, (clip_count, D), jnp.float32)
    spread = 1.0 + 2.0 * position
    blend = 1.5 * position
    mixture = (noise_part + blend[:, None] * common[clip_id]) * (spread / jnp.sqrt(1.0 + blend * blend))[:, None]
    return mixture.astype(jnp.bfloat16)


def block_scale(own_key, dims, cuts, least, top_value):
    def one(dim, parts):
        draws = jax.random.uniform(jax.random.fold_in(jax.random.fold_in(own_key, 6), dim), (parts,), jnp.float32, least / len(cuts), top_value / len(cuts))
        return jnp.repeat(jnp.exp(draws), dims[dim] // parts).reshape((-1,) + (1,) * (len(dims) - dim - 1))

    loudness = one(*cuts[0])
    for cut in cuts[1:]:
        loudness = loudness * one(*cut)
    return loudness


def scatter_about(stream_key, dims, width, reach, cuts=(), kind=jnp.bfloat16):
    values = jax.random.normal(stream_key, dims, jnp.float32) * width
    if len(cuts) > 0:
        values = block_scale(stream_key, dims, cuts, -0.22, 0.18) * values
    return jnp.clip(values, min=-reach, max=reach).astype(kind)


def setup_inputs(seed: int = 0) -> dict:
    key_of = jax.random.split(jax.random.key(seed), 14)
    return {
        "tokens": draw_tokens(jax.random.fold_in(key_of[13], 71), 0),
        "cotangent": scatter_about(key_of[1], (TOKENS, D), 1.0, 6.0, ((0, 32),)),
        "ln_gain": jnp.clip(1.0 + 0.18 * jax.random.normal(key_of[2], (3, D), jnp.float32), 0.1, 1.9),
        "ln_bias": scatter_about(key_of[3], (3, D), 0.5, 3.0, ((1, 32),), jnp.float32),
        "out_bias": scatter_about(key_of[4], (3, D), 0.5, 3.0, ((1, 32),), jnp.float32),
        "qv_bias": scatter_about(key_of[5], (4, D), 0.5, 3.0, ((1, 32),), jnp.float32),
        "up_bias": scatter_about(key_of[6], (FF,), 0.5, 3.0, ((0, 32),), jnp.float32),
        "qkv_spatial": scatter_about(key_of[7], (3, D, D), D ** -0.5, 0.21875, ((1, 8), (2, 4))),
        "out_spatial": scatter_about(key_of[8], (D, D), (D // 8) ** -0.5, 0.625, ((0, 4), (1, 8))),
        "qkv_temporal": scatter_about(key_of[9], (3, D, D), D ** -0.5, 0.21875, ((1, 8), (2, 4))),
        "out_temporal": scatter_about(key_of[10], (D, D), (D // 2) ** -0.5, 0.3125, ((0, 4), (1, 8))),
        "up_weight": scatter_about(key_of[11], (D, FF), D ** -0.5, 0.21875, ((0, 8), (1, 4))),
        "down_weight": scatter_about(key_of[12], (FF, D), FF ** -0.5, 0.109375, ((0, 4), (1, 8))),
    }


EPS = 1e-06
PRECISE = lax.Precision.HIGHEST

@jax.custom_vjp
def low(v):
    return lax.optimization_barrier(v.astype(jnp.bfloat16)).astype(jnp.float32)

@jax.custom_vjp
def low_back(v):
    return v

def low_keep(v):
    return (low(v), None)

def low_pass(kept, grad):
    return (grad,)

def back_keep(v):
    return (v, None)

def back_low(kept, grad):
    return (low(grad),)
low.defvjp(low_keep, low_pass)
low_back.defvjp(back_keep, back_low)

def both_ways(value):
    return low(low_back(value))

def normalize(stream, gain_row, shift_row):
    average = lax.optimization_barrier(jnp.mean(stream, axis=-1, keepdims=True))
    centered = stream - average
    variance = lax.optimization_barrier(jnp.mean(centered * centered, axis=-1, keepdims=True))
    return centered * lax.rsqrt(variance + EPS) * gain_row + shift_row

def linear(inputs, weights):
    return jnp.einsum('...d,dw->...w', inputs, weights, precision=PRECISE)

def attention(inputs, weights, query_bias, value_bias, out_weight, out_row, score_form, mix_form):
    head_shape = inputs.shape[:-1] + (HEADS, HD)
    queries = both_ways(linear(inputs, weights[0]) + query_bias).reshape(head_shape)
    key_rows = both_ways(linear(inputs, weights[1])).reshape(head_shape)
    value_rows = both_ways(linear(inputs, weights[2]) + value_bias).reshape(head_shape)
    scores = low_back(jnp.einsum(score_form, queries, key_rows, precision=PRECISE)) * HD ** (-0.5)
    probability = low(jax.nn.softmax(scores, axis=-1))
    mixture = jnp.einsum(mix_form, probability, value_rows, precision=PRECISE).reshape(inputs.shape)
    mixture = both_ways(mixture)
    return low_back(linear(mixture, out_weight) + out_row)

def block(stream, params):
    gains, shifts, out_rows, qv_rows, up_row, spatial_w, spatial_out, temporal_w, temporal_out, up_w, down_w = params
    input_first = low(normalize(stream, gains[0], shifts[0]))
    spatial = attention(input_first, spatial_w, qv_rows[0], qv_rows[1], spatial_out, out_rows[0], 'cfphe,cfqhe->cfhpq', 'cfhpq,cfqhe->cfphe')
    stream_first = stream + spatial
    input_second = low(normalize(stream_first, gains[1], shifts[1]))
    temporal = attention(input_second, temporal_w, qv_rows[2], qv_rows[3], temporal_out, out_rows[1], 'cfphe,cgphe->cphfg', 'cphfg,cgphe->cfphe')
    stream_second = stream_first + temporal
    input_third = low(normalize(stream_second, gains[2], shifts[2]))
    pre_act = low_back(linear(input_third, up_w) + up_row)
    hidden = low(jax.nn.gelu(pre_act, approximate=True))
    branch = low_back(linear(hidden, down_w) + out_rows[2])
    stream_third = stream_second + branch
    squares = jnp.stack([jnp.sum(stream_third * stream_third), jnp.sum(spatial * spatial), jnp.sum(temporal * temporal), jnp.sum(branch * branch)])
    return (stream_third, squares)

def arrange(values):
    pairs = values.shape[0] // (CLIPS * FRAMES * PLACES)
    shaped = values.reshape(pairs, 2, CLIPS, FRAMES // 2, PLACES, values.shape[-1])
    return shaped.transpose(0, 2, 1, 3, 4, 5).reshape(pairs, CLIPS, FRAMES, PLACES, values.shape[-1])

def restore(values):
    pairs = values.shape[0]
    shaped = values.reshape(pairs, CLIPS, 2, FRAMES // 2, PLACES, values.shape[-1])
    return shaped.transpose(0, 2, 1, 3, 4, 5).reshape(-1, values.shape[-1])

def reference(tokens, cotangent, ln_gain, ln_bias, out_bias, qv_bias, up_bias, qkv_spatial, out_spatial, qkv_temporal, out_temporal, up_weight, down_weight):
    params = tuple((argument.astype(jnp.float32) for argument in (ln_gain, ln_bias, out_bias, qv_bias, up_bias, qkv_spatial, out_spatial, qkv_temporal, out_temporal, up_weight, down_weight)))
    inputs = arrange(tokens.astype(jnp.float32))
    cotangents = arrange(cotangent.astype(jnp.float32))
    zero_grads = jax.tree.map(jnp.zeros_like, params)

    def one_pair(running, pieces):
        grad_sums, totals = running
        stream, grad_out = pieces
        result, pullback, squares = jax.vjp(block, stream, params, has_aux=True)
        grad_in, grad_params = pullback(grad_out)
        grad_sums = jax.tree.map(jnp.add, grad_sums, grad_params)
        return ((grad_sums, totals + squares), (result, grad_in))
    (grads, totals), (outputs, input_grads) = lax.scan(one_pair, (zero_grads, jnp.zeros((4,), jnp.float32)), (inputs, cotangents))
    entries = tokens.shape[0] * tokens.shape[1]
    root_means = jnp.sqrt(totals / entries)
    return (restore(outputs).astype(jnp.bfloat16), restore(input_grads), grads[0], grads[1], grads[2], grads[3], grads[4], grads[5], grads[6], grads[7], grads[8], grads[9], grads[10], root_means)
```

```python
import math

import jax
import jax.numpy as jnp
from jax import lax
from jax.experimental import pallas as pl
from jax.experimental.pallas import tpu as pltpu
from jax.sharding import PartitionSpec as P

HD = 64
FRAMES = 8
PLACES = 196
D = 768
EPS = 1e-06
QUART = PLACES // 4
PADP = 208
ROWS = 2 * PLACES
PROWS = 2 * PADP
GROUPS = 4
COLORS = ("byax", "abyx", "byxa", "axyb", "axby", "baxy")
BLOCKS = ((0, 128), (128, 128), (256, 136))
BF = jnp.bfloat16
F32 = jnp.float32
SCALE = HD**-0.5
GELU_A = math.sqrt(2.0 / math.pi)
GELU_B = 0.044715


class Net:
    def __init__(self, fsdp, tp):
        self.size = {"fsdp": fsdp, "tp": tp}
        self.fbits = fsdp.bit_length() - 1
        names = "yab" if self.fbits == 3 else None
        self.where = {"c": ("tp", 0), "x": ("tp", 1)}
        for i in range(self.fbits):
            self.where[names[i] if names else f"f{i}"] = ("fsdp", i)
        self.dims = [d for d in self.where if d != "c"]
        self.fdims = [d for d in self.dims if d != "x"]
        if self.fbits == 3:
            self.orders = [list(o) for o in COLORS]
        else:
            n = len(self.dims)
            self.orders = [[self.dims[(i + c) % n] for i in range(n)] for c in range(6)]

    def swap(self, block, dim):
        axis, bit = self.where[dim]
        return lax.ppermute(block, axis, [(i, i ^ (1 << bit)) for i in range(self.size[axis])])


def together(*values):
    return lax.optimization_barrier(values)


def gather_all(net, own, small):
    rows = own.shape[0] // 6
    held = [own[rows * c : rows * (c + 1)][None] for c in range(6)]
    steps = len(net.dims)
    small = small[None]
    small = jnp.concatenate([small, net.swap(small, "c")], 0)
    for step in range(steps):
        jobs = {}
        for c, order in enumerate(net.orders):
            jobs.setdefault(order[step], []).append(c)
        got = [None] * 6
        n = held[0].shape[0]
        for dim, cs in jobs.items():
            block = jnp.concatenate([held[c] for c in cs], 0) if len(cs) > 1 else held[cs[0]]
            came = net.swap(block, dim)
            for k, c in enumerate(cs):
                got[c] = came[k * n : (k + 1) * n]
        more = net.swap(small, net.dims[step])
        out = together(*held, *got, small, more)
        held = [jnp.concatenate([h, v], 0) for h, v in zip(out[:6], out[6:12])]
        small = jnp.concatenate([out[12], out[13]], 0)
    full = jnp.stack(held, 0)
    return full, net.swap(full, "c"), small


def relative_order(net, order):
    out = []
    for i in range(2 ** len(order)):
        f = x = 0
        for k, dim in enumerate(order):
            if i >> k & 1:
                axis, bit = net.where[dim]
                if axis == "fsdp":
                    f |= 1 << bit
                else:
                    x = 1
        out.append((f, x))
    return out


def plain_weights(net, full, other, fi, ti):
    fsdp = net.size["fsdp"]
    rows = full.shape[2]
    per_core = []
    for held in (full, other):
        colors = []
        for c, order in enumerate(net.orders):
            place = {fx: i for i, fx in enumerate(relative_order(net, order))}
            idx = jnp.array([[place[(f, x)] for f in range(fsdp)] for x in range(2)])
            colors.append(held[c][idx.reshape(-1)].reshape(2, fsdp, rows, D))
        per_core.append(jnp.concatenate(colors, 2))
    every = jnp.stack(per_core, 1).reshape(4, fsdp, 6 * rows, D)
    every = every[jnp.arange(4) ^ ti][:, jnp.arange(fsdp) ^ fi]
    every = every.reshape(4, fsdp, GROUPS, 6 * rows // GROUPS, D)
    return every.transpose(2, 0, 1, 3, 4).reshape(GROUPS, 4, D, D)


def scatter_sum(net, keep, send):
    rows = keep.shape[2]
    part = rows // 6

    def add(a, b):
        return (a.astype(F32) + b.astype(F32)).astype(BF)

    whole = add(keep, net.swap(send, "c"))
    shape = (2,) * len(net.dims)
    axes = ["x"] + net.fdims[::-1]
    held = [
        whole[:, :, part * c : part * (c + 1)].reshape(shape + (part, D)) for c in range(6)
    ]
    left = [list(axes) for _ in range(6)]
    steps = len(net.dims)
    for step in range(steps):
        jobs = {}
        for c, order in enumerate(net.orders):
            jobs.setdefault(order[steps - 1 - step], []).append(c)
        got, kept = [None] * 6, [None] * 6
        for dim, cs in jobs.items():
            sends = []
            for c in cs:
                at = left[c].index(dim)
                kept[c] = lax.index_in_dim(held[c], 0, at, keepdims=False)
                sends.append(lax.index_in_dim(held[c], 1, at, keepdims=False).reshape(-1, part, D))
                left[c].pop(at)
            block = jnp.concatenate(sends, 0) if len(sends) > 1 else sends[0]
            came = net.swap(block, dim)
            n = sends[0].shape[0]
            for k, c in enumerate(cs):
                got[c] = came[k * n : (k + 1) * n].reshape(kept[c].shape)
        out = together(*kept, *got)
        held = [add(k, g) for k, g in zip(out[:6], out[6:])]
    return jnp.concatenate(held, 0)


def sum_all(net, value):
    for dim in ["c"] + net.dims:
        value = value + net.swap(value, dim)
    return value


def exchange(net, pieces):
    one = net.swap(pieces[1], "c")
    dim = net.fdims[0]
    tp, fsdp = net.size["tp"], net.size["fsdp"]
    two = net.swap(pieces[2], dim)
    route = [(f * tp + t, (f ^ 1) * tp + (t ^ 1)) for f in range(fsdp) for t in range(tp)]
    three = lax.ppermute(pieces[3], ("fsdp", "tp"), route)
    return jnp.stack([pieces[0], one, two, three], 0)


def nn(a, b):
    return lax.dot_general(a, b, (((1,), (0,)), ((), ())), preferred_element_type=F32)


def nt(a, b):
    return lax.dot_general(a, b, (((1,), (1,)), ((), ())), preferred_element_type=F32)


def tn(a, b):
    return lax.dot_general(a, b, (((0,), (0,)), ((), ())), preferred_element_type=F32)


def fetch(net, me, srcs, group, w, sem):
    if len(srcs) == 1:
        copy = pltpu.make_async_copy(srcs[0].at[group], w, sem)
        copy.start()
        return copy.wait
    fi, ti = me[0], me[1]
    for core, src in enumerate(srcs):
        for unit in range(3 * group, 3 * group + 3):
            color, half, part = unit // 2, unit % 2, unit % 3
            for i, (f, x) in enumerate(relative_order(net, net.orders[color])):
                row = pl.multiple_of((f ^ fi) * 96 + 32 * part, 32)
                pltpu.make_async_copy(
                    src.at[color, i, pl.ds(32 * half, 32)],
                    w.at[(2 * x + core) ^ ti, pl.ds(row, 32)],
                    sem,
                ).start()
    return pltpu.make_async_copy(w, w, sem).wait


def emit(net, me, t, value, refs, col, width):
    if len(refs) == 1:
        refs[0][t, :, pl.ds(col, width)] = value.astype(BF)
        return
    fi, ti = me[0], me[1]
    r = t ^ ti
    value = value.astype(BF)
    for core, ref in enumerate(refs):

        @pl.when((r & 1) == core)
        def _(ref=ref):
            for f in range(8):
                ref[r >> 1, f ^ fi, :, pl.ds(col, width)] = value[96 * f : 96 * (f + 1)]


def norm_of(x):
    centered = x - jnp.mean(x, axis=-1, keepdims=True)
    r = lax.rsqrt(jnp.mean(centered * centered, axis=-1, keepdims=True) + EPS)
    return centered * r, r


def norm_back(da, xhat, r, gain):
    t = da * gain
    return r * (t - jnp.mean(t, -1, keepdims=True) - xhat * jnp.mean(t * xhat, -1, keepdims=True))


def colsum(x):
    return jnp.sum(x, axis=0, keepdims=True)


def total(x):
    return jnp.sum(jnp.sum(x, axis=0, keepdims=True), axis=1, keepdims=True)


def softmax_of(s, mask):
    s = jnp.where(mask, s * SCALE, -1e30)
    e = jnp.exp(s - jnp.max(s, axis=-1, keepdims=True))
    return (e / jnp.sum(e, axis=-1, keepdims=True)).astype(BF)


def attend_back(q, k, v, p, do):
    dv = tn(p, do)
    dp = nt(do, v)
    pf = p.astype(F32)
    delta = jnp.sum(dp * pf, axis=-1, keepdims=True)
    ds = (pf * (dp - delta) * SCALE).astype(BF)
    return nn(ds, k), tn(ds, q), dv


def spread(came, lanes):
    for j in range(8):
        value = came[j // 2, j % 2].astype(F32)
        for n in range(D // 128):
            lanes[n, pl.ds(j, QUART, stride=8), :] = value[:, 128 * n : 128 * (n + 1)]
    return jnp.concatenate([lanes[n] for n in range(D // 128)], 1)


def collect(value, lanes, out):
    for n in range(D // 128):
        lanes[n] = value[:, 128 * n : 128 * (n + 1)]
    for j in range(8):
        out[j // 2, j % 2] = jnp.concatenate(
            [lanes[n, pl.ds(j, QUART, stride=8), :] for n in range(D // 128)], 1
        ).astype(BF)


def spatial_fwd(net, packed, me, tok, vec, qkvb, *refs):
    srcs, (u_out, qkv, o, p, sums, w, a, u, sem) = refs[:packed], refs[packed:]
    wait = fetch(net, me, srcs, 0, w, sem)
    xhat, _ = norm_of(tok[...].astype(F32))
    a[...] = (xhat * vec[0:1] + vec[3:4]).astype(BF)
    wait()
    u[...] = jnp.zeros_like(u)
    valid = lax.broadcasted_iota(jnp.int32, (PADP, PADP), 1) < PLACES

    def per_tp(t, _):
        qkv[t] = (nn(a[...], w[t, :, 0:576]) + qkvb[t]).astype(BF)
        for h in range(3):
            for f in range(2):
                rows = slice(PADP * f, PADP * (f + 1))
                q, k, v = (qkv[t, rows, 192 * j + HD * h : 192 * j + HD * (h + 1)] for j in range(3))
                prob = softmax_of(nt(q, k), valid)
                p[t, h, f] = prob
                o[t, rows, HD * h : HD * (h + 1)] = nn(prob, v).astype(BF)
        u[...] += nt(o[t], w[t, :, 576:768])
        return 0

    lax.fori_loop(0, 4, per_tp, 0)
    value = u[...] + vec[6:7]
    u[...] = value
    row = lax.broadcasted_iota(jnp.int32, (PROWS, D), 0)
    real = (row < PLACES) | ((row >= PADP) & (row < PADP + PLACES))
    sums[...] = jnp.broadcast_to(total(jnp.where(real, value * value, 0.0)), sums.shape)
    for d in range(4):
        for f in range(2):
            u_out[me[2] ^ d, f] = u[PADP * f + QUART * d : PADP * f + QUART * (d + 1), :].astype(BF)


def temporal_fwd(net, packed, me, tok, came, vec, qkvb, *refs):
    srcs, (h1, h2, qkv, o, p, sums, w, a, u, lanes, sem) = refs[:packed], refs[packed:]
    wait = fetch(net, me, srcs, 1, w, sem)
    h1[...] = spread(came, lanes) + tok[...].astype(F32)
    xhat, _ = norm_of(h1[...])
    a[...] = (xhat * vec[1:2] + vec[4:5]).astype(BF)
    wait()
    u[...] = jnp.zeros_like(u)

    def per_tp(t, _):
        qkv[t] = (nn(a[...], w[t, :, 0:576]) + qkvb[t]).astype(BF)
        for start, n in BLOCKS:
            rows = slice(start, start + n)
            row = lax.broadcasted_iota(jnp.int32, (n, n), 0) >> 3
            col = lax.broadcasted_iota(jnp.int32, (n, n), 1) >> 3
            for h in range(3):
                q, k, v = (qkv[t, rows, 192 * j + HD * h : 192 * j + HD * (h + 1)] for j in range(3))
                prob = softmax_of(nt(q, k), row == col)
                p[t, h, rows, 0:n] = prob
                o[t, rows, HD * h : HD * (h + 1)] = nn(prob, v).astype(BF)
        u[...] += nt(o[t], w[t, :, 576:768])
        return 0

    lax.fori_loop(0, 4, per_tp, 0)
    value = u[...] + vec[7:8]
    sums[...] = jnp.broadcast_to(total(value * value), sums.shape)
    h2[...] = h1[...] + value


def mlp_both(net, packed, outs, me, h2, cot, vec, upb, *refs):
    srcs, refs = refs[:packed], refs[packed:]
    dup, ddown = refs[:outs], refs[outs : 2 * outs]
    h3, e2, dupb, vgrad, sums, wu, wd, a, at, ct, u, da, lanes, sem = refs[2 * outs :]
    waits = [fetch(net, me, srcs, 2, wu, sem.at[0]), fetch(net, me, srcs, 3, wd, sem.at[1])]
    xhat, r = norm_of(h2[...])
    a3 = xhat * vec[2:3] + vec[5:6]
    a[...] = a3.astype(BF)
    at[...] = a3.T.astype(BF)
    ct[...] = cot[...].astype(F32).T.astype(BF)
    u[...] = jnp.zeros_like(u)
    da[...] = jnp.zeros_like(da)
    for wait in waits:
        wait()

    def per_tp(t, _):
        z = nn(a[...], wu[t]) + upb[t]
        zz = z * z
        th = jnp.tanh(GELU_A * (z + GELU_B * zz * z))
        g = (0.5 * z * (1.0 + th)).astype(BF)
        slope = 0.5 * (1.0 + th) + (0.5 * GELU_A) * z * (1.0 - th * th) * (1.0 + (3.0 * GELU_B) * zz)
        u[...] += nt(g, wd[t])
        dz = (nn(cot[...], wd[t]) * slope).astype(BF)
        dupb[t] = colsum(dz.astype(F32))
        emit(net, me, t, nn(ct[...], g), ddown, 0, D)
        emit(net, me, t, nn(at[...], dz), dup, 0, D)
        da[...] += nt(dz, wu[t])
        return 0

    lax.fori_loop(0, 4, per_tp, 0)
    value = u[...] + vec[8:9]
    out = h2[...] + value
    sums[0:1] = jnp.broadcast_to(total(value * value), (1, 128))
    sums[1:2] = jnp.broadcast_to(total(out * out), (1, 128))
    collect(out, lanes, h3)
    xhat, r = norm_of(h2[...])
    grad = da[...]
    vgrad[0:1] = colsum(grad * xhat)
    vgrad[1:2] = colsum(grad)
    vgrad[2:3] = colsum(cot[...].astype(F32))
    e2[...] = cot[...].astype(F32) + norm_back(grad, xhat, r, vec[2:3])


def temporal_bwd(net, packed, outs, me, e2, h1, cot, qkv, o, p, vec, *refs):
    srcs, refs = refs[:packed], refs[packed:]
    dws = refs[:outs]
    back, dqkvb, vgrad, w, c, at, ct, do, dqkv, da, lanes, sem = refs[outs:]
    wait = fetch(net, me, srcs, 1, w, sem)
    xhat, r = norm_of(h1[...])
    at[...] = (xhat * vec[1:2] + vec[4:5]).T.astype(BF)
    c[...] = e2[...].astype(BF)
    cf = c[...].astype(F32)
    ct[...] = cf.T.astype(BF)
    vgrad[2:3] = colsum(cf)
    da[...] = jnp.zeros_like(da)
    wait()

    def per_tp(t, _):
        do[...] = nn(c[...], w[t, :, 576:768]).astype(BF)
        for start, n in BLOCKS:
            rows = slice(start, start + n)
            for h in range(3):
                q, k, v = (qkv[t, rows, 192 * j + HD * h : 192 * j + HD * (h + 1)] for j in range(3))
                three = attend_back(q, k, v, p[t, h, rows, 0:n], do[rows, HD * h : HD * (h + 1)])
                for j, part in enumerate(three):
                    dqkv[rows, 192 * j + HD * h : 192 * j + HD * (h + 1)] = part.astype(BF)
        dqkvb[t] = colsum(dqkv[...].astype(F32))
        emit(net, me, t, jnp.concatenate([nn(at[...], dqkv[...]), nn(ct[...], o[t])], 1), dws, 0, D)
        da[...] += nt(dqkv[...], w[t, :, 0:576])
        return 0

    lax.fori_loop(0, 4, per_tp, 0)
    xhat, r = norm_of(h1[...])
    grad = da[...]
    vgrad[0:1] = colsum(grad * xhat)
    vgrad[1:2] = colsum(grad)
    collect(e2[...] + norm_back(grad, xhat, r, vec[1:2]) - cot[...].astype(F32), lanes, back)


def spatial_bwd(net, packed, outs, me, came, cot, tok, qkv, o, p, vec, *refs):
    srcs, refs = refs[:packed], refs[packed:]
    dws = refs[:outs]
    gin, dqkvb, vgrad, w, four, e1, c, at, ct, do, dqkv, da, sem = refs[outs:]
    wait = fetch(net, me, srcs, 0, w, sem)
    for k in range(4):
        for f in range(2):
            four[me[2] ^ k, f] = came[k, f].astype(F32)
    e1[...] = jnp.zeros_like(e1)
    for d in range(4):
        for f in range(2):
            e1[PADP * f + QUART * d : PADP * f + QUART * (d + 1), :] = four[d, f]
    e1[...] += cot[...].astype(F32)
    xhat, r = norm_of(tok[...].astype(F32))
    at[...] = (xhat * vec[0:1] + vec[3:4]).T.astype(BF)
    c[...] = e1[...].astype(BF)
    cf = c[...].astype(F32)
    ct[...] = cf.T.astype(BF)
    vgrad[2:3] = colsum(cf)
    da[...] = jnp.zeros_like(da)
    wait()

    def per_tp(t, _):
        do[...] = nn(c[...], w[t, :, 576:768]).astype(BF)
        for f in range(2):
            rows = slice(PADP * f, PADP * (f + 1))
            for h in range(3):
                q, k, v = (qkv[t, rows, 192 * j + HD * h : 192 * j + HD * (h + 1)] for j in range(3))
                three = attend_back(q, k, v, p[t, h, f], do[rows, HD * h : HD * (h + 1)])
                for j, part in enumerate(three):
                    dqkv[rows, 192 * j + HD * h : 192 * j + HD * (h + 1)] = part.astype(BF)
        dqkvb[t] = colsum(dqkv[...].astype(F32))
        emit(net, me, t, jnp.concatenate([nn(at[...], dqkv[...]), nn(ct[...], o[t])], 1), dws, 0, D)
        da[...] += nt(dqkv[...], w[t, :, 0:576])
        return 0

    lax.fori_loop(0, 4, per_tp, 0)
    xhat, r = norm_of(tok[...].astype(F32))
    grad = da[...]
    vgrad[0:1] = colsum(grad * xhat)
    vgrad[1:2] = colsum(grad)
    da[...] = e1[...] + norm_back(grad, xhat, r, vec[0:1])
    for f in range(2):
        gin[PLACES * f : PLACES * (f + 1), :] = da[PADP * f : PADP * f + PLACES, :]


def call(kernel, me, ins, srcs, outs, scratch, flops):
    smem, vmem, any_ = (pl.BlockSpec(memory_space=s) for s in (pltpu.SMEM, pltpu.VMEM, pl.ANY))
    moved = sum(math.prod(v.shape) * v.dtype.itemsize for v in ins) + sum(
        math.prod(s) * jnp.dtype(t).itemsize for s, t in outs
    )
    return pl.pallas_call(
        kernel,
        out_shape=[jax.ShapeDtypeStruct(s, t) for s, t in outs],
        in_specs=[smem] + [vmem] * len(ins) + [any_] * len(srcs),
        out_specs=[vmem] * len(outs),
        scratch_shapes=scratch,
        compiler_params=pltpu.CompilerParams(vmem_limit_bytes=60 * 1024 * 1024),
        cost_estimate=pl.CostEstimate(
            flops=flops, transcendentals=0, bytes_accessed=moved + GROUPS * D * D * 2
        ),
        name=kernel.func.__name__,
    )(me, *ins, *srcs)


def bind(kernel, *static):
    import functools

    return functools.partial(kernel, *static)


def scattered(net, fast, outs, fi, ti):
    if fast:
        return outs
    fsdp = net.size["fsdp"]
    grad = outs[0].reshape(4, fsdp, D // fsdp, D)
    grad = grad[jnp.arange(4) ^ ti][:, jnp.arange(fsdp) ^ fi].reshape(2, 2, fsdp, D // fsdp, D)
    return grad[:, 0], grad[:, 1]


def on_device(fsdp, tp, *args):
    tokens, cotangent, ln_gain, ln_bias, out_bias, qv_bias, up_bias = args[:7]
    qkv_spatial, out_spatial, qkv_temporal, out_temporal, up_weight, down_weight = args[7:]
    net = Net(fsdp, tp)
    fast = fsdp == 8
    span = D // fsdp
    fi, ti = lax.axis_index("fsdp"), lax.axis_index("tp")
    me4 = 2 * (fi & 1) + (ti & 1)
    me = jnp.stack([fi, ti, me4]).astype(jnp.int32)

    own = jnp.concatenate(
        [
            jnp.concatenate([qkv_spatial[0], qkv_spatial[1], qkv_spatial[2], out_spatial.T], 1),
            jnp.concatenate([qkv_temporal[0], qkv_temporal[1], qkv_temporal[2], out_temporal.T], 1),
            up_weight,
            down_weight.T,
        ],
        0,
    )
    world = fsdp * tp
    part, upart = D // world, up_bias.shape[0]
    flat = jnp.concatenate(
        [ln_gain.reshape(-1), ln_bias.reshape(-1), out_bias.reshape(-1), qv_bias.reshape(-1), up_bias]
    )
    small = jnp.pad(flat, (0, -flat.shape[0] % 128)).reshape(-1, 128)

    def to_pieces(rows):
        four = rows.reshape(2, 4, QUART, D).transpose(1, 0, 2, 3)
        return four[me4 ^ jnp.arange(4)]

    def to_rows(pieces):
        return pieces.reshape(8, QUART, D).transpose(1, 0, 2).reshape(ROWS, D)

    both = jnp.stack([to_pieces(tokens), to_pieces(cotangent)], 1)
    both = exchange(net, both)
    tok_t, cot_t = to_rows(both[:, 0]), to_rows(both[:, 1])
    pad = lambda rows: jnp.pad(rows.reshape(2, PLACES, D), ((0, 0), (0, PADP - PLACES), (0, 0))).reshape(PROWS, D)
    tok_p, cot_p = pad(tokens), pad(cotangent)

    own, small, tok_t, cot_t = together(own, small, tok_t, cot_t)
    full, other, small = gather_all(net, own, small)
    idx = [0] * world
    for i in range(world):
        f, t = 0, i & 1
        for k, dim in enumerate(net.dims):
            if i >> (k + 1) & 1:
                axis, bit = net.where[dim]
                if axis == "fsdp":
                    f |= 1 << bit
                else:
                    t |= 1 << bit
        idx[f * tp + t] = i
    small = small.reshape(world, -1)[jnp.array(idx)]
    small = small[jnp.arange(world) ^ (fi * tp + ti)]
    vec = small[:, : 13 * part].reshape(world, 13, part).transpose(1, 0, 2).reshape(13, D)
    upb = small[:, 13 * part : 13 * part + upart].reshape(4, 1, D)
    qv = vec[9:13].reshape(4, 4, 192)
    zero = jnp.zeros((4, 192), F32)
    qkvb_s = jnp.concatenate([qv[0], zero, qv[1]], 1)[:, None]
    qkvb_t = jnp.concatenate([qv[2], zero, qv[3]], 1)[:, None]

    if fast:
        srcs = [full, other]
    else:
        srcs = [plain_weights(net, full, other, fi, ti)]
    packed = len(srcs)
    gshape = [((2, fsdp, span, D), BF)] * 2 if fast else [((4, D, D), BF)]
    outs = len(gshape)
    V, S = pltpu.VMEM, pltpu.SemaphoreType.DMA
    wbuf = V((4, D, D), BF)
    lanes = V((D // 128, ROWS, 128), F32)
    pieces = ((4, 2, QUART, D), BF)

    u1, qkv1, o1, p1, sum1 = call(
        bind(spatial_fwd, net, packed),
        me,
        [tok_p, vec, qkvb_s],
        srcs,
        [
            pieces,
            ((4, PROWS, 576), BF),
            ((4, PROWS, 192), BF),
            ((4, 3, 2, PADP, PADP), BF),
            ((1, 128), F32),
        ],
        [wbuf, V((PROWS, D), BF), V((PROWS, D), F32), S(())],
        2 * PROWS * D * D * 4,
    )
    u1 = exchange(net, u1)
    h1, h2, qkv2, o2, p2, sum2 = call(
        bind(temporal_fwd, net, packed),
        me,
        [tok_t, u1, vec, qkvb_t],
        srcs,
        [
            ((ROWS, D), F32),
            ((ROWS, D), F32),
            ((4, ROWS, 576), BF),
            ((4, ROWS, 192), BF),
            ((4, 3, ROWS, 136), BF),
            ((1, 128), F32),
        ],
        [wbuf, V((ROWS, D), BF), V((ROWS, D), F32), lanes, S(())],
        2 * ROWS * D * D * 4,
    )
    res = call(
        bind(mlp_both, net, packed, outs),
        me,
        [h2, cot_t, vec, upb],
        srcs,
        gshape
        + gshape
        + [pieces, ((ROWS, D), F32), ((4, 1, D), F32), ((3, D), F32), ((2, 128), F32)],
        [wbuf, wbuf, V((ROWS, D), BF), V((D, ROWS), BF), V((D, ROWS), BF)]
        + [V((ROWS, D), F32)] * 2
        + [lanes]
        + [S((2,))],
        2 * ROWS * D * D * 24,
    )
    dup, ddown = res[:outs], res[outs : 2 * outs]
    h3, e2, dupb, vg3, sum3 = res[2 * outs :]
    res = call(
        bind(temporal_bwd, net, packed, outs),
        me,
        [e2, h1, cot_t, qkv2, o2, p2, vec],
        srcs,
        gshape + [pieces, ((4, 1, 576), F32), ((3, D), F32)],
        [
            wbuf,
            V((ROWS, D), BF),
            V((D, ROWS), BF),
            V((D, ROWS), BF),
            V((ROWS, 192), BF),
            V((ROWS, 576), BF),
            V((ROWS, D), F32),
            lanes,
            S(()),
        ],
        2 * ROWS * D * D * 8,
    )
    dtemp = res[:outs]
    back, dqkvb2, vg2 = res[outs:]
    back = exchange(net, back)
    res = call(
        bind(spatial_bwd, net, packed, outs),
        me,
        [back, cot_p, tok_p, qkv1, o1, p1, vec],
        srcs,
        gshape + [((ROWS, D), F32), ((4, 1, 576), F32), ((3, D), F32)],
        [
            wbuf,
            V((4, 2, QUART, D), F32),
            V((PROWS, D), F32),
            V((PROWS, D), BF),
            V((D, PROWS), BF),
            V((D, PROWS), BF),
            V((PROWS, 192), BF),
            V((PROWS, 576), BF),
            V((PROWS, D), F32),
            S(()),
        ],
        2 * PROWS * D * D * 8,
    )
    dspat = res[:outs]
    input_grad, dqkvb1, vg1 = res[outs:]

    h3 = exchange(net, h3)
    output = h3[me4 ^ jnp.arange(4)].transpose(1, 0, 2, 3).reshape(ROWS, D)

    def pair(a, b):
        a, b = scattered(net, fast, a, fi, ti), scattered(net, fast, b, fi, ti)
        return scatter_sum(net, jnp.concatenate([a[0], b[0]], 2), jnp.concatenate([a[1], b[1]], 2))

    mlp = pair(dup, ddown)
    attn = pair(dtemp, dspat)
    up_g, down_g = mlp[:span].astype(F32), mlp[span:].astype(F32).T
    temp, spat = attn[:span].astype(F32), attn[span:].astype(F32)

    def apart(grad):
        return jnp.stack([grad[:, 0:192], grad[:, 192:384], grad[:, 384:576]], 0), grad[:, 576:768].T

    spat_g, spat_out_g = apart(spat)
    temp_g, temp_out_g = apart(temp)

    def qv_rows(g):
        return jnp.stack([g[:, 0, 0:192].reshape(D), g[:, 0, 384:576].reshape(D)], 0)

    sums = jnp.stack([sum3[1, 0], sum1[0, 0], sum2[0, 0], sum3[0, 0]])
    rows = jnp.concatenate(
        [
            jnp.stack([vg1[0], vg2[0], vg3[0], vg1[1], vg2[1], vg3[1], vg1[2], vg2[2], vg3[2]], 0),
            qv_rows(dqkvb1),
            qv_rows(dqkvb2),
            dupb[:, 0],
            jnp.pad(sums, (0, D - 4))[None],
        ],
        0,
    )
    rows = sum_all(net, rows)
    at = fi * tp + ti
    mine = lax.dynamic_slice_in_dim(rows[:13], at * part, part, 1)
    up_b = lax.dynamic_slice_in_dim(rows[13:17].reshape(-1), at * upart, upart, 0)
    entries = tokens.shape[0] * D * world
    root_means = jnp.sqrt(rows[17, :4] / entries)
    return (
        output,
        input_grad,
        mine[0:3],
        mine[3:6],
        mine[6:9],
        mine[9:13],
        up_b,
        spat_g,
        spat_out_g,
        temp_g,
        temp_out_g,
        up_g,
        down_g,
        root_means,
    )


def solution(mesh):
    rows = P(("fsdp", "tp"), None)
    lanes = P(None, ("fsdp", "tp"))
    specs = (rows, rows, lanes, lanes, lanes, lanes, P(("fsdp", "tp")))
    weights = (
        P(None, "fsdp", "tp"),
        P("tp", "fsdp"),
        P(None, "fsdp", "tp"),
        P("tp", "fsdp"),
        P("fsdp", "tp"),
        P("tp", "fsdp"),
    )
    fsdp, tp = mesh.shape["fsdp"], mesh.shape["tp"]

    def body(*args):
        return on_device(fsdp, tp, *args)

    return jax.shard_map(
        body,
        mesh=mesh,
        in_specs=specs + weights,
        out_specs=specs + weights + (P(),),
        check_vma=False,
    )
```
